32 devices in a mesh: pair: 8 (over y, x, core), occ: 4 (over z).
Axes of the slice: x: 2, y: 2, z: 4, core: 2. Of those that a mesh axis runs over, the one named last changes fastest.
Arguments:
- half_ints: bfloat16 [4, 3072, 6144], P('occ', 'pair'), may hold values from -6 to 6
- pair_coef: bfloat16 [512, 3072], P('occ'), may hold values from -0.15625 to 0.15625
- mo_virtual: bfloat16 [5632, 6144], P('pair'), may hold values from -0.078125 to 0.078125
- screen: int32 [48], replicated, may hold values 0 or 1
- slot_block: int32 [48], replicated, may hold values from 0 to 47, each once
Outputs:
- mo_block: bfloat16 [5632, 4, 512], P('pair', 'occ')
The draws below stay inside these ranges and needn't reach their ends.
Inputs may be any that keep to these rules, and one draw needn't show every extreme that they name: `screen`: 1 where the pair block survives screening, 0 where it is dropped. `slot_block`: each logical pair block stands in exactly one storage slot; index k of pair holds slots k * 6 to k * 6 + 5.
All inputs are finite; a program needn't handle non-finite values.
Results may differ from the reference program's by a relative error of at most 0.0049.
Values may be sent and summed in bfloat16 or wider, within the bound.
A program may use at most 128 MiB of HBM per device.

```python
import jax
import jax.numpy as jnp
from jax import lax

NB = 6144
NV = 5632
J = 512
BLK = 64
NPB = 48
NQ = 3072
I = 4


def with_ends(array, own_key, least, high):
    extent = array.shape
    spot = [jax.random.randint(jax.random.fold_in(own_key, axis), (), 0, extent[axis]) for axis in range(len(extent))]
    array = array.at[tuple(spot)].set(least)
    longest = extent.index(max(extent))
    spot[longest] = (spot[longest] + 1) % extent[longest]
    return array.at[tuple(spot)].set(high)


def block_levels(own_key, shape, shards, least, high):
    gain = 1.0
    for position, parts in shards:
        draws = jax.random.uniform(jax.random.fold_in(jax.random.fold_in(own_key, 6), position), (parts,), jnp.float32, least / len(shards), high / len(shards))
        gain = gain * jnp.repeat(jnp.exp(draws), shape[position] // parts).reshape((-1,) + (1,) * (len(shape) - 1 - position))
    return gain


def gaussian(own_key, dims, deviation, bound, split=(), held_as=jnp.bfloat16):
    entries = jax.random.normal(own_key, dims, jnp.float32) * deviation
    if len(split) > 0:
        entries = block_levels(own_key, dims, split, -0.22, 0.18) * entries
    return jnp.clip(entries, min=-bound, max=bound).astype(held_as)


def setup_inputs(seed: int = 0) -> dict:
    keys = jax.random.split(jax.random.key(seed), 6)
    return {
        "half_ints": gaussian(keys[0], (I, NQ, NB), 1.0, 6.0, ((0, 4), (1, 8))),
        "pair_coef": gaussian(keys[1], (J, NQ), (NQ // 2) ** -0.5, 0.15625, ((0, 4),)),
        "mo_virtual": gaussian(keys[2], (NV, NB), NB ** -0.5, 0.078125, ((0, 8),)),
        "screen": with_ends((jax.random.randint(keys[3], (NPB,), 0, 2) < 1).astype(jnp.int32), jax.random.fold_in(keys[3], 1), 0, 1),
        "slot_block": jax.random.permutation(keys[4], NPB).astype(jnp.int32),
    }


def reference(half_ints, pair_coef, mo_virtual, screen, slot_block):
    masked_coef = pair_coef.reshape(J, NPB, BLK) * screen.astype(jnp.bfloat16)[None, :, None]
    selected = jnp.take(masked_coef, slot_block.astype(jnp.int32), axis=1).reshape(J, NQ)

    def one_orbital(ints_row):
        occ_pair = jnp.dot(selected, ints_row, preferred_element_type=jnp.float32).astype(jnp.bfloat16)
        return jnp.dot(mo_virtual, occ_pair.T, preferred_element_type=jnp.float32).astype(jnp.bfloat16)

    stacked = lax.map(one_orbital, half_ints)
    return jnp.transpose(stacked, (1, 0, 2))
```

```python
import functools

import jax
import jax.numpy as jnp
from jax import lax
from jax.experimental import pallas as pl
from jax.experimental.pallas import tpu as pltpu
from jax.sharding import PartitionSpec as P

MESH = pl.DeviceIdType.MESH
WIDTH = 1024
VMEM = 56 * 2**20
REDUCE = 2, 4
GATHER = 3, 4
FINISH = 1


def flip(index, stride):
    return index + stride * (1 - 2 * (lax.rem(lax.div(index, stride), 2)))


def flip_by(index, mask):
    for bit in range(mask.bit_length()):
        if (mask >> bit) & 1:
            index = flip(index, 1 << bit)
    return index


def xor(a, b, bits):
    total = 0
    for bit in range(bits):
        total = total + lax.rem(lax.div(a, 1 << bit) + lax.div(b, 1 << bit), 2) * (1 << bit)
    return total


def kernel(
    n_pair, n_occ, block,
    half_hbm, coef_hbm, virt_hbm, screen_hbm, slot_hbm,
    out_ref,
    coef_buf, half_buf, sel_buf, virt_buf, part, kept, gathered, twin, total,
    screen_ref, slot_ref, *rest,
):
    steps = n_pair.bit_length() - 2
    landed, sems = rest[:steps], rest[steps:]
    (name_sem, coef_sem, half_local, half_send, half_recv, sel_send, sel_recv, pass_send, pass_recv,
     virt_sem, rs_send, rs_recv, ag_send, ag_recv, twin_send, twin_recv) = sems
    me = lax.axis_index("pair")
    z = lax.axis_index("occ")
    core = lax.rem(me, 2)
    other = flip(me, 1)
    subs, _, width = half_buf.shape
    chunks, rows, _ = part.shape
    depth = half_hbm.shape[0]
    half_n = subs * width

    up = [2 << s for s in range(steps)]
    down = up[steps // 2:] + up[:steps // 2]
    stride = [a + core * (b - a) for a, b in zip(up, down)]
    partner = [flip(me, s) for s in stride]
    keep, send = [], []
    r0, c0, r, c = 0, 0, rows, width
    for s in range(steps):
        bit = lax.rem(lax.div(me, stride[s]), 2)
        if r >= 32:
            r = r // 2
            kr, kc, sr, sc = r0 + bit * r, c0, r0 + (1 - bit) * r, c0
        else:
            c = c // 2
            kr, kc, sr, sc = r0, c0 + bit * c, r0, c0 + (1 - bit) * c
        region = lambda a, b, r=r, c=c: (
            pl.ds(a if isinstance(a, int) else pl.multiple_of(a, 16), r),
            pl.ds(b if isinstance(b, int) else pl.multiple_of(b, 128), c),
        )
        keep.append(region(kr, kc))
        send.append(region(sr, sc))
        r0, c0 = kr, kc

    def half_copy(k):
        own = half_hbm.at[:, pl.ds(pl.multiple_of(core * half_n + k * width, 128), width)]
        dst = half_buf.at[k, pl.ds(pl.multiple_of(core * depth, 16), depth), :]
        return pltpu.make_async_copy(own, dst, half_local)

    def half_remote(k):
        src = half_hbm.at[:, pl.ds(pl.multiple_of((1 - core) * half_n + k * width, 128), width)]
        dst = half_buf.at[k, pl.ds(pl.multiple_of(core * depth, 16), depth), :]
        return pltpu.make_async_remote_copy(
            src, dst, half_send, half_recv.at[k], device_id={"pair": other}, device_id_type=MESH)

    mine = pl.ds(pl.multiple_of(core * (rows // 2), 16), rows // 2)

    def sel_remote(hop, way):
        origin = sel_buf.at[z - way * hop, mine]
        return pltpu.make_async_remote_copy(
            origin, origin, sel_send.at[hop, (way + 1) // 2], sel_recv.at[z - way * hop],
            device_id={"occ": z + way}, device_id_type=MESH)

    def sel_pass(hop, way):
        origin = sel_buf.at[z - way * hop, mine]
        return pltpu.make_async_remote_copy(
            origin, origin, pass_send.at[hop, (way + 1) // 2], pass_recv.at[z - way * hop],
            device_id={"pair": other}, device_id_type=MESH)

    def sel_arrival(sem, origin, half):
        block = sel_buf.at[origin, half]
        return pltpu.make_async_remote_copy(
            block, block, sel_send.at[0, 0], sem.at[origin],
            device_id={"pair": other}, device_id_type=MESH)

    def inside(place):
        return (place >= 0) & (place < n_occ)

    def rs_remote(s, t):
        return pltpu.make_async_remote_copy(
            part.at[(t, *send[s])], landed[s].at[t], rs_send.at[s], rs_recv.at[s, t],
            device_id={"pair": partner[s]}, device_id_type=MESH)

    def ag_remote(s, t):
        return pltpu.make_async_remote_copy(
            gathered.at[(t, *keep[s])], gathered.at[(t, *keep[s])], ag_send.at[s], ag_recv.at[s, t],
            device_id={"pair": partner[s]}, device_id_type=MESH)

    def ag_arrival(s, t):
        return pltpu.make_async_remote_copy(
            gathered.at[(t, *send[s])], gathered.at[(t, *send[s])], ag_send.at[s], ag_recv.at[s, t],
            device_id={"pair": partner[s]}, device_id_type=MESH)

    def twin_remote(t):
        return pltpu.make_async_remote_copy(
            gathered.at[t], twin.at[t], twin_send, twin_recv.at[t],
            device_id={"pair": other}, device_id_type=MESH)

    def coef_copy(k):
        src = coef_hbm.at[:, pl.ds(pl.multiple_of(k * 128, 128), 128)]
        return pltpu.make_async_copy(src, coef_buf.at[k], coef_sem)

    virt_copy = pltpu.make_async_copy(virt_hbm, virt_buf, virt_sem)

    barrier = pltpu.get_barrier_semaphore()
    pl.semaphore_signal(barrier, inc=1, device_id={"pair": other}, device_id_type=MESH)
    for s in range(steps):
        pl.semaphore_signal(barrier, inc=1, device_id={"pair": partner[s]}, device_id_type=MESH)
    for way in (-1, 1):
        @pl.when(inside(z + way))
        def _():
            pl.semaphore_signal(barrier, inc=1, device_id={"occ": z + way}, device_id_type=MESH)

    tiles = coef_buf.shape[0]
    names = [
        pltpu.make_async_copy(screen_hbm, screen_ref, name_sem.at[0]),
        pltpu.make_async_copy(slot_hbm, slot_ref, name_sem.at[1]),
    ]
    for copy in names:
        copy.start()

    def fetch(k, _):
        coef_copy(k).start()
        return 0

    lax.fori_loop(0, tiles, fetch, 0)
    for k in range(subs):
        half_copy(k).start()
    total[...] = jnp.zeros_like(total)
    for copy in names:
        copy.wait()
    pltpu.make_async_copy(coef_buf, coef_buf, coef_sem).wait()

    per = 128 // block
    slots = 2 * depth // block
    chip = lax.div(me, 2)
    lane = lax.broadcasted_iota(jnp.int32, (rows, 128), 1)
    for pos in range(slots // per):
        tile = jnp.zeros((rows, 128), jnp.float32)
        for spot in range(per):
            name = slot_ref[chip * slots + pos * per + spot]
            keepit = screen_ref[name].astype(jnp.float32)
            at = lax.rem(name, per)
            got = coef_buf[lax.div(name, per)].astype(jnp.float32) * keepit
            for shift in range(per):
                moved = pltpu.roll(got, shift * block, 1) if shift else got
                here = (lax.rem(at + shift, per) == spot).astype(jnp.float32)
                tile = tile + jnp.where(lax.div(lane, block) == spot, moved, 0.0) * here
        sel_buf[z, :, pos * 128:(pos + 1) * 128] = tile.astype(jnp.bfloat16)

    pl.semaphore_wait(barrier, 1 + steps + inside(z - 1).astype(jnp.int32) + inside(z + 1).astype(jnp.int32))
    for k in range(subs):
        half_remote(k).start()
    for way in (-1, 1):
        @pl.when(inside(z + way))
        def _():
            sel_remote(0, way).start()

    def relay(hop):
        for way in (-1, 1):
            origin = z - way * hop

            @pl.when(inside(origin))
            def _():
                sel_arrival(sel_recv, origin, mine).wait_recv()

                @pl.when(inside(z + way))
                def _():
                    sel_remote(hop, way).start()

                sel_pass(hop, way).start()

    def produce(t):
        d, k = lax.div(t, subs), lax.rem(t, subs)

        origin = xor(z, d, (n_occ - 1).bit_length())

        @pl.when(t == 0)
        def _():
            for k in range(subs):
                half_copy(k).wait()

        @pl.when(d == 0)
        def _():
            half_remote(k).wait_recv()

        @pl.when((d > 0) & (k == 0))
        def _():
            theirs = pl.ds(pl.multiple_of((1 - core) * (rows // 2), 16), rows // 2)
            sel_arrival(pass_recv, origin, theirs).wait_recv()

        p = jnp.dot(sel_buf[origin], half_buf[k], preferred_element_type=jnp.float32)
        kept[t] = p
        part[t] = p.astype(jnp.bfloat16)
        rs_remote(0, t).start()

    def reduce(s, t):
        rs_remote(s, t).wait_recv()
        v = kept[(t, *keep[s])] + landed[s][t].astype(jnp.float32)
        if s + 1 < steps:
            kept[(t, *keep[s])] = v
            part[(t, *keep[s])] = v.astype(jnp.bfloat16)
            rs_remote(s + 1, t).start()
        else:
            gathered[(t, *keep[s])] = v.astype(jnp.bfloat16)
            ag_remote(s, t).start()

    def fold(t, buf, side):
        d, k = lax.div(t, subs), lax.rem(t, subs)
        cols = pl.ds(pl.multiple_of(side * half_n + k * width, 128), width)
        total[d] += lax.dot_general(
            virt_buf[:, cols], buf[t], (((1,), (1,)), ((), ())), preferred_element_type=jnp.float32)

    def gather(s, t):
        ag_arrival(s, t).wait_recv()
        if s > 0:
            ag_remote(s - 1, t).start()
        else:
            twin_remote(t).start()
            fold(t, gathered, core)

    def finish(t):
        twin_remote(t).wait_recv()
        fold(t, twin, 1 - core)
        d, k = lax.div(t, subs), lax.rem(t, subs)
        origin = xor(z, d, (n_occ - 1).bit_length())

        @pl.when(k == subs - 1)
        def _():
            if len(out_ref.shape) == 2:
                cols = pl.ds(pl.multiple_of(origin * rows, 128), rows)
                out_ref[:, cols] = total[d].astype(jnp.bfloat16)
            else:
                out_ref[origin] = total[d].astype(jnp.bfloat16)

    stages = [functools.partial(reduce, s) for s in range(steps)]
    stages += [functools.partial(gather, s) for s in reversed(range(steps))]
    stages += [finish]
    gaps = [REDUCE[min(s, 1)] for s in range(steps)]
    gaps += [GATHER[0]] + [GATHER[1]] * (steps - 1) + [FINISH]
    delay = [sum(gaps[:i + 1]) for i in range(len(gaps))]

    def body(t, _):
        @pl.when(t < chunks)
        def _():
            produce(t)

        @pl.when(t == subs)
        def _():
            virt_copy.start()

        @pl.when(t == delay[-2])
        def _():
            virt_copy.wait()

        for stage, late in zip(stages, delay):
            u = t - late

            @pl.when((u >= 0) & (u < chunks))
            def _():
                stage(u)

        for hop in range(1, n_occ):
            @pl.when(t == hop * subs - 1)
            def _():
                relay(hop)
        return 0

    lax.fori_loop(0, chunks + delay[-1], body, 0)

    half_all = half_hbm.at[:, pl.ds(0, half_n)]
    pltpu.make_async_remote_copy(
        half_all, half_all, half_send, half_recv.at[0], device_id={"pair": other}, device_id_type=MESH).wait_send()
    for hop in range(n_occ):
        for way in (-1, 1):
            @pl.when(inside(z - way * hop) & inside(z + way))
            def _():
                sel_remote(hop, way).wait_send()

            if hop:
                @pl.when(inside(z - way * hop))
                def _():
                    sel_pass(hop, way).wait_send()
    for s in range(steps):
        for sem in (rs_send, ag_send):
            pltpu.make_async_remote_copy(
                landed[s], landed[s], sem.at[s], rs_recv.at[s, 0],
                device_id={"pair": partner[s]}, device_id_type=MESH).wait_send()
    pltpu.make_async_remote_copy(
        gathered, twin, twin_send, twin_recv.at[0], device_id={"pair": other}, device_id_type=MESH).wait_send()


def shards(n_pair, n_occ, half_ints, pair_coef, mo_virtual, screen, slot_block):
    rows = pair_coef.shape[0]
    basis = half_ints.shape[2]
    depth = half_ints.shape[1]
    half_ints = half_ints.reshape(depth, basis)
    block = pair_coef.shape[1] // screen.shape[0]
    width = min(WIDTH, basis // 2)
    subs = basis // 2 // width
    chunks = subs * n_occ
    virt = mo_virtual.shape[0]
    steps = n_pair.bit_length() - 2
    tiles = pair_coef.shape[1] // 128
    wide = rows % 128 == 0
    landed = []
    r, c = rows, width
    for _ in range(steps):
        r, c = (r // 2, c) if r >= 32 else (r, c // 2)
        landed.append(pltpu.VMEM((chunks, r, c), jnp.bfloat16))
    dma = pltpu.SemaphoreType.DMA
    out = pl.pallas_call(
        functools.partial(kernel, n_pair, n_occ, block),
        out_shape=pltpu.VMEM(
            (virt, n_occ * rows) if wide else (n_occ, virt, rows), jnp.bfloat16),
        in_specs=[pl.BlockSpec(memory_space=pltpu.HBM)] * 5,
        out_specs=pl.BlockSpec(memory_space=pltpu.VMEM),
        scratch_shapes=[
            pltpu.VMEM((tiles, rows, 128), jnp.bfloat16),
            pltpu.VMEM((subs, 2 * depth, width), jnp.bfloat16),
            pltpu.VMEM((n_occ, rows, 2 * depth), jnp.bfloat16),
            pltpu.VMEM((virt, basis), jnp.bfloat16),
            pltpu.VMEM((chunks, rows, width), jnp.bfloat16),
            pltpu.VMEM((chunks, rows, width), jnp.float32),
            pltpu.VMEM((chunks, rows, width), jnp.bfloat16),
            pltpu.VMEM((chunks, rows, width), jnp.bfloat16),
            pltpu.VMEM((n_occ, virt, rows), jnp.float32),
            pltpu.SMEM(screen.shape, jnp.int32),
            pltpu.SMEM(slot_block.shape, jnp.int32),
            *landed,
            dma((2,)), dma, dma, dma, dma((subs,)),
            dma((n_occ, 2)), dma((n_occ,)), dma((n_occ, 2)), dma((n_occ,)), dma,
            dma((steps,)), dma((steps, chunks)), dma((steps,)), dma((steps, chunks)),
            dma, dma((chunks,)),
        ],
        compiler_params=pltpu.CompilerParams(
            collective_id=0, has_side_effects=True, vmem_limit_bytes=VMEM),
    )(half_ints, pair_coef, mo_virtual, screen, slot_block)
    if not wide:
        out = jnp.transpose(out, (1, 0, 2))
    return out.reshape(virt, 1, n_occ * rows)


def solution(mesh):
    placed = (P("occ", "pair", None), P("occ", None), P("pair", None), P(), P())
    return jax.shard_map(
        functools.partial(shards, mesh.shape["pair"], mesh.shape["occ"]),
        mesh=mesh, in_specs=placed, out_specs=P("pair", "occ", None), check_vma=False,
    )
```

```python
import functools

import jax
import jax.numpy as jnp
from jax import lax
from jax.experimental import pallas as pl
from jax.experimental.pallas import tpu as pltpu
from jax.sharding import PartitionSpec as P

MESH = pl.DeviceIdType.MESH
WIDTH = 1024
PIECE = 256
VMEM = 56 * 2**20
REDUCE = 2, 4
GATHER = 3, 4
FINISH = 1


def flip(index, stride):
    return index + stride * (1 - 2 * (lax.rem(lax.div(index, stride), 2)))


def flip_by(index, mask):
    for bit in range(mask.bit_length()):
        if (mask >> bit) & 1:
            index = flip(index, 1 << bit)
    return index


def xor(a, b, bits):
    total = 0
    for bit in range(bits):
        total = total + lax.rem(lax.div(a, 1 << bit) + lax.div(b, 1 << bit), 2) * (1 << bit)
    return total


def kernel(
    n_pair, n_occ, block,
    half_hbm, coef_hbm, virt_hbm, screen_hbm, slot_hbm,
    out_ref,
    coef_buf, half_buf, sel_buf, virt_buf, part, kept, gathered, twin, total,
    screen_ref, slot_ref, *rest,
):
    steps = n_pair.bit_length() - 2
    landed, sems = rest[:steps], rest[steps:]
    (name_sem, coef_sem, half_local, half_send, half_recv, sel_send, sel_recv, pass_send, pass_recv,
     virt_sem, rs_send, rs_recv, ag_send, ag_recv, twin_send, twin_recv) = sems
    me = lax.axis_index("pair")
    z = lax.axis_index("occ")
    core = lax.rem(me, 2)
    other = flip(me, 1)
    subs, _, width = half_buf.shape
    chunks, rows, _ = part.shape
    depth = half_hbm.shape[0]
    half_n = subs * width

    up = [2 << s for s in range(steps)]
    down = up[steps // 2:] + up[:steps // 2]
    stride = [a + core * (b - a) for a, b in zip(up, down)]
    partner = [flip(me, s) for s in stride]
    keep, send = [], []
    r0, c0, r, c = 0, 0, rows, width
    for s in range(steps):
        bit = lax.rem(lax.div(me, stride[s]), 2)
        if r >= 32:
            r = r // 2
            kr, kc, sr, sc = r0 + bit * r, c0, r0 + (1 - bit) * r, c0
        else:
            c = c // 2
            kr, kc, sr, sc = r0, c0 + bit * c, r0, c0 + (1 - bit) * c
        region = lambda a, b, r=r, c=c: (
            pl.ds(a if isinstance(a, int) else pl.multiple_of(a, 16), r),
            pl.ds(b if isinstance(b, int) else pl.multiple_of(b, 128), c),
        )
        keep.append(region(kr, kc))
        send.append(region(sr, sc))
        r0, c0 = kr, kc

    def half_copy(k):
        own = half_hbm.at[:, pl.ds(pl.multiple_of(core * half_n + k * width, 128), width)]
        dst = half_buf.at[k, pl.ds(pl.multiple_of(core * depth, 16), depth), :]
        return pltpu.make_async_copy(own, dst, half_local)

    pieces = half_recv.shape[0] // subs
    piece = width // pieces

    def half_remote(k, q):
        src = half_hbm.at[:, pl.ds(pl.multiple_of((1 - core) * half_n + k * width + q * piece, 128), piece)]
        dst = half_buf.at[k, pl.ds(pl.multiple_of(core * depth, 16), depth), q * piece:(q + 1) * piece]
        return pltpu.make_async_remote_copy(
            src, dst, half_send, half_recv.at[k * pieces + q], device_id={"pair": other}, device_id_type=MESH)

    mine = pl.ds(pl.multiple_of(core * (rows // 2), 16), rows // 2)

    def sel_remote(hop, way):
        origin = sel_buf.at[z - way * hop, mine]
        return pltpu.make_async_remote_copy(
            origin, origin, sel_send.at[hop, (way + 1) // 2], sel_recv.at[z - way * hop],
            device_id={"occ": z + way}, device_id_type=MESH)

    def sel_pass(hop, way):
        origin = sel_buf.at[z - way * hop, mine]
        return pltpu.make_async_remote_copy(
            origin, origin, pass_send, pass_recv.at[z - way * hop],
            device_id={"pair": other}, device_id_type=MESH)

    def sel_arrival(sem, origin, half):
        block = sel_buf.at[origin, half]
        return pltpu.make_async_remote_copy(
            block, block, sel_send.at[0, 0], sem.at[origin],
            device_id={"pair": other}, device_id_type=MESH)

    def inside(place):
        return (place >= 0) & (place < n_occ)

    def rs_remote(s, t):
        return pltpu.make_async_remote_copy(
            part.at[(t, *send[s])], landed[s].at[t], rs_send.at[s], rs_recv.at[s, t],
            device_id={"pair": partner[s]}, device_id_type=MESH)

    def rs_piece(t, q):
        if pieces == 1:
            return rs_remote(0, t)
        cols = slice(q * piece, (q + 1) * piece)
        return pltpu.make_async_remote_copy(
            part.at[t, send[0][0], cols], landed[0].at[t, :, cols], rs_send.at[0], rs_recv.at[0, t],
            device_id={"pair": partner[0]}, device_id_type=MESH)

    def ag_remote(s, t):
        return pltpu.make_async_remote_copy(
            gathered.at[(t, *keep[s])], gathered.at[(t, *keep[s])], ag_send.at[s], ag_recv.at[s, t],
            device_id={"pair": partner[s]}, device_id_type=MESH)

    def ag_arrival(s, t):
        return pltpu.make_async_remote_copy(
            gathered.at[(t, *send[s])], gathered.at[(t, *send[s])], ag_send.at[s], ag_recv.at[s, t],
            device_id={"pair": partner[s]}, device_id_type=MESH)

    def twin_part(t, region):
        return pltpu.make_async_remote_copy(
            gathered.at[(t, *region)], twin.at[(t, *region)], twin_send, twin_recv.at[t],
            device_id={"pair": other}, device_id_type=MESH)

    def twin_remote(t):
        return pltpu.make_async_remote_copy(
            gathered.at[t], twin.at[t], twin_send, twin_recv.at[t],
            device_id={"pair": other}, device_id_type=MESH)

    def coef_copy(k):
        src = coef_hbm.at[:, pl.ds(pl.multiple_of(k * 128, 128), 128)]
        return pltpu.make_async_copy(src, coef_buf.at[k], coef_sem)

    virt_copy = pltpu.make_async_copy(virt_hbm, virt_buf, virt_sem)

    barrier = pltpu.get_barrier_semaphore()
    pl.semaphore_signal(barrier, inc=1, device_id={"pair": other}, device_id_type=MESH)
    for s in range(steps):
        pl.semaphore_signal(barrier, inc=1, device_id={"pair": partner[s]}, device_id_type=MESH)
    for way in (-1, 1):
        @pl.when(inside(z + way))
        def _():
            pl.semaphore_signal(barrier, inc=1, device_id={"occ": z + way}, device_id_type=MESH)

    tiles = coef_buf.shape[0]
    names = [
        pltpu.make_async_copy(screen_hbm, screen_ref, name_sem.at[0]),
        pltpu.make_async_copy(slot_hbm, slot_ref, name_sem.at[1]),
    ]
    for copy in names:
        copy.start()

    def fetch(k, _):
        coef_copy(k).start()
        return 0

    lax.fori_loop(0, tiles, fetch, 0)
    for k in range(subs):
        half_copy(k).start()

    pl.semaphore_wait(barrier, 1 + steps + inside(z - 1).astype(jnp.int32) + inside(z + 1).astype(jnp.int32))
    for k in range(subs):
        for q in range(pieces):
            half_remote(k, q).start()

    for copy in names:
        copy.wait()
    pltpu.make_async_copy(coef_buf, coef_buf, coef_sem).wait()

    per = 128 // block
    slots = 2 * depth // block
    chip = lax.div(me, 2)
    lane = lax.broadcasted_iota(jnp.int32, (rows, 128), 1)
    for pos in range(slots // per):
        tile = jnp.zeros((rows, 128), jnp.float32)
        for spot in range(per):
            name = slot_ref[chip * slots + pos * per + spot]
            keepit = screen_ref[name].astype(jnp.float32)
            at = lax.rem(name, per)
            got = coef_buf[lax.div(name, per)].astype(jnp.float32) * keepit
            for shift in range(per):
                moved = pltpu.roll(got, shift * block, 1) if shift else got
                here = (lax.rem(at + shift, per) == spot).astype(jnp.float32)
                tile = tile + jnp.where(lax.div(lane, block) == spot, moved, 0.0) * here
        sel_buf[z, :, pos * 128:(pos + 1) * 128] = tile.astype(jnp.bfloat16)

    for way in (-1, 1):
        @pl.when(inside(z + way))
        def _():
            sel_remote(0, way).start()

    def relay(hop):
        for way in (-1, 1):
            origin = z - way * hop

            @pl.when(inside(origin))
            def _():
                sel_arrival(sel_recv, origin, mine).wait_recv()

                @pl.when(inside(z + way))
                def _():
                    sel_remote(hop, way).start()

                sel_pass(hop, way).start()

    def produce(t):
        d, k = lax.div(t, subs), lax.rem(t, subs)

        origin = xor(z, d, (n_occ - 1).bit_length())

        @pl.when(t == 0)
        def _():
            for k in range(subs):
                half_copy(k).wait()

        def make(q, part_of):
            cols = slice(q * part_of, (q + 1) * part_of)
            p = jnp.dot(sel_buf[origin], half_buf[k, :, cols], preferred_element_type=jnp.float32)
            kept[t, :, cols] = p
            part[t, :, cols] = p.astype(jnp.bfloat16)

        @pl.when(d == 0)
        def _():
            for q in range(pieces):
                half_remote(k, q).wait_recv()
                make(q, piece)
                rs_piece(t, q).start()

        @pl.when((d > 0) & (k == 0))
        def _():
            theirs = pl.ds(pl.multiple_of((1 - core) * (rows // 2), 16), rows // 2)
            sel_arrival(pass_recv, origin, theirs).wait_recv()

        @pl.when(d > 0)
        def _():
            make(0, width)
            rs_remote(0, t).start()

    def reduce(s, t):
        rs_remote(s, t).wait_recv()
        v = kept[(t, *keep[s])] + landed[s][t].astype(jnp.float32)
        if s + 1 < steps:
            kept[(t, *keep[s])] = v
            part[(t, *keep[s])] = v.astype(jnp.bfloat16)
            rs_remote(s + 1, t).start()
        else:
            gathered[(t, *keep[s])] = v.astype(jnp.bfloat16)
            ag_remote(s, t).start()
            twin_part(t, keep[s]).start()

    def fold(t, buf, side):
        d, k = lax.div(t, subs), lax.rem(t, subs)
        cols = pl.ds(pl.multiple_of(side * half_n + k * width, 128), width)
        total[d] += lax.dot_general(
            virt_buf[:, cols], buf[t], (((1,), (1,)), ((), ())), preferred_element_type=jnp.float32)

    def gather(s, t):
        ag_arrival(s, t).wait_recv()
        if s > 0:
            ag_remote(s - 1, t).start()
        twin_part(t, send[s]).start()
        if s == 0:
            fold(t, gathered, core)

    def finish(t):
        twin_remote(t).wait_recv()
        fold(t, twin, 1 - core)
        d, k = lax.div(t, subs), lax.rem(t, subs)
        origin = xor(z, d, (n_occ - 1).bit_length())

        @pl.when(k == subs - 1)
        def _():
            if len(out_ref.shape) == 2:
                cols = pl.ds(pl.multiple_of(origin * rows, 128), rows)
                out_ref[:, cols] = total[d].astype(jnp.bfloat16)
            else:
                out_ref[origin] = total[d].astype(jnp.bfloat16)

    stages = [functools.partial(reduce, s) for s in range(steps)]
    stages += [functools.partial(gather, s) for s in reversed(range(steps))]
    stages += [finish]
    gaps = [REDUCE[min(s, 1)] for s in range(steps)]
    gaps += [GATHER[0]] + [GATHER[1]] * (steps - 1) + [FINISH]
    delay = [sum(gaps[:i + 1]) for i in range(len(gaps))]

    def body(t, _):
        @pl.when(t < chunks)
        def _():
            produce(t)

        @pl.when(t == subs)
        def _():
            virt_copy.start()
            total[...] = jnp.zeros_like(total)

        @pl.when(t == delay[-2])
        def _():
            virt_copy.wait()

        for stage, late in zip(stages, delay):
            u = t - late

            @pl.when((u >= 0) & (u < chunks))
            def _():
                stage(u)

        for hop in range(1, n_occ):
            @pl.when(t == hop * subs - 1)
            def _():
                relay(hop)
        return 0

    lax.fori_loop(0, chunks + delay[-1], body, 0)

    half_all = half_hbm.at[:, pl.ds(0, half_n)]
    pltpu.make_async_remote_copy(
        half_all, half_all, half_send, half_recv.at[0], device_id={"pair": other}, device_id_type=MESH).wait_send()
    for hop in range(n_occ):
        for way in (-1, 1):
            @pl.when(inside(z - way * hop) & inside(z + way))
            def _():
                sel_remote(hop, way).wait_send()

    passed = sel_buf.at[pl.ds(0, n_occ - 1), mine]
    pltpu.make_async_remote_copy(
        passed, passed, pass_send, pass_recv.at[0], device_id={"pair": other}, device_id_type=MESH).wait_send()
    for s in range(steps):
        for sem in (rs_send, ag_send):
            pltpu.make_async_remote_copy(
                landed[s], landed[s], sem.at[s], rs_recv.at[s, 0],
                device_id={"pair": partner[s]}, device_id_type=MESH).wait_send()
    pltpu.make_async_remote_copy(
        gathered, twin, twin_send, twin_recv.at[0], device_id={"pair": other}, device_id_type=MESH).wait_send()


def shards(n_pair, n_occ, half_ints, pair_coef, mo_virtual, screen, slot_block):
    rows = pair_coef.shape[0]
    basis = half_ints.shape[2]
    depth = half_ints.shape[1]
    half_ints = half_ints.reshape(depth, basis)
    block = pair_coef.shape[1] // screen.shape[0]
    width = min(WIDTH, basis // 2)
    subs = basis // 2 // width
    chunks = subs * n_occ
    virt = mo_virtual.shape[0]
    steps = n_pair.bit_length() - 2
    tiles = pair_coef.shape[1] // 128
    wide = rows % 128 == 0
    landed = []
    r, c = rows, width
    for _ in range(steps):
        r, c = (r // 2, c) if r >= 32 else (r, c // 2)
        landed.append(pltpu.VMEM((chunks, r, c), jnp.bfloat16))
    dma = pltpu.SemaphoreType.DMA
    out = pl.pallas_call(
        functools.partial(kernel, n_pair, n_occ, block),
        out_shape=pltpu.VMEM(
            (virt, n_occ * rows) if wide else (n_occ, virt, rows), jnp.bfloat16),
        in_specs=[pl.BlockSpec(memory_space=pltpu.HBM)] * 5,
        out_specs=pl.BlockSpec(memory_space=pltpu.VMEM),
        scratch_shapes=[
            pltpu.VMEM((tiles, rows, 128), jnp.bfloat16),
            pltpu.VMEM((subs, 2 * depth, width), jnp.bfloat16),
            pltpu.VMEM((n_occ, rows, 2 * depth), jnp.bfloat16),
            pltpu.VMEM((virt, basis), jnp.bfloat16),
            pltpu.VMEM((chunks, rows, width), jnp.bfloat16),
            pltpu.VMEM((chunks, rows, width), jnp.float32),
            pltpu.VMEM((chunks, rows, width), jnp.bfloat16),
            pltpu.VMEM((chunks, rows, width), jnp.bfloat16),
            pltpu.VMEM((n_occ, virt, rows), jnp.float32),
            pltpu.SMEM(screen.shape, jnp.int32),
            pltpu.SMEM(slot_block.shape, jnp.int32),
            *landed,
            dma((2,)), dma, dma, dma, dma((subs * (width // PIECE if rows >= 32 and width % PIECE == 0 else 1),)),
            dma((n_occ, 2)), dma((n_occ,)), dma, dma((n_occ,)), dma,
            dma((steps,)), dma((steps, chunks)), dma((steps,)), dma((steps, chunks)),
            dma, dma((chunks,)),
        ],
        compiler_params=pltpu.CompilerParams(
            collective_id=0, has_side_effects=True, vmem_limit_bytes=VMEM),
    )(half_ints, pair_coef, mo_virtual, screen, slot_block)
    if not wide:
        out = jnp.transpose(out, (1, 0, 2))
    return out.reshape(virt, 1, n_occ * rows)


def solution(mesh):
    placed = (P("occ", "pair", None), P("occ", None), P("pair", None), P(), P())
    return jax.shard_map(
        functools.partial(shards, mesh.shape["pair"], mesh.shape["occ"]),
        mesh=mesh, in_specs=placed, out_specs=P("pair", "occ", None), check_vma=False,
    )
```

```python
import functools

import jax
import jax.numpy as jnp
from jax import lax
from jax.experimental import pallas as pl
from jax.experimental.pallas import tpu as pltpu
from jax.sharding import PartitionSpec as P

MESH = pl.DeviceIdType.MESH
WIDTH = 1024
PIECE = 256
EARLY = 1
VMEM = 56 * 2**20
REDUCE = 2, 3
GATHER = 3, 3
FINISH = 1


def flip(index, stride):
    return index + stride * (1 - 2 * (lax.rem(lax.div(index, stride), 2)))


def flip_by(index, mask):
    for bit in range(mask.bit_length()):
        if (mask >> bit) & 1:
            index = flip(index, 1 << bit)
    return index


def xor(a, b, bits):
    total = 0
    for bit in range(bits):
        total = total + lax.rem(lax.div(a, 1 << bit) + lax.div(b, 1 << bit), 2) * (1 << bit)
    return total


def kernel(
    n_pair, n_occ, block,
    half_hbm, coef_hbm, virt_hbm, screen_hbm, slot_hbm,
    out_ref,
    coef_buf, half_buf, sel_buf, virt_buf, part, kept, gathered, twin, total,
    screen_ref, slot_ref, *rest,
):
    steps = n_pair.bit_length() - 2
    landed, sems = rest[:steps], rest[steps:]
    (name_sem, coef_sem, half_local, half_send, half_recv, sel_send, sel_recv, pass_send, pass_recv,
     virt_sem, rs_send, rs_recv, ag_send, ag_recv, twin_send, twin_recv) = sems
    me = lax.axis_index("pair")
    z = lax.axis_index("occ")
    core = lax.rem(me, 2)
    other = flip(me, 1)
    subs, _, width = half_buf.shape
    chunks, rows, _ = part.shape
    depth = half_hbm.shape[0]
    half_n = subs * width

    up = [2 << s for s in range(steps)]
    down = up[steps // 2:] + up[:steps // 2]
    stride = [a + core * (b - a) for a, b in zip(up, down)]
    partner = [flip(me, s) for s in stride]
    keep, send = [], []
    r0, c0, r, c = 0, 0, rows, width
    for s in range(steps):
        bit = lax.rem(lax.div(me, stride[s]), 2)
        if r >= 32:
            r = r // 2
            kr, kc, sr, sc = r0 + bit * r, c0, r0 + (1 - bit) * r, c0
        else:
            c = c // 2
            kr, kc, sr, sc = r0, c0 + bit * c, r0, c0 + (1 - bit) * c
        region = lambda a, b, r=r, c=c: (
            pl.ds(a if isinstance(a, int) else pl.multiple_of(a, 16), r),
            pl.ds(b if isinstance(b, int) else pl.multiple_of(b, 128), c),
        )
        keep.append(region(kr, kc))
        send.append(region(sr, sc))
        r0, c0 = kr, kc

    def half_copy(k):
        own = half_hbm.at[:, pl.ds(pl.multiple_of(core * half_n + k * width, 128), width)]
        dst = half_buf.at[k, pl.ds(pl.multiple_of(core * depth, 16), depth), :]
        return pltpu.make_async_copy(own, dst, half_local)

    pieces = half_recv.shape[0] // subs
    piece = width // pieces

    def half_remote(k, q):
        src = half_hbm.at[:, pl.ds(pl.multiple_of((1 - core) * half_n + k * width + q * piece, 128), piece)]
        dst = half_buf.at[k, pl.ds(pl.multiple_of(core * depth, 16), depth), q * piece:(q + 1) * piece]
        return pltpu.make_async_remote_copy(
            src, dst, half_send, half_recv.at[k * pieces + q], device_id={"pair": other}, device_id_type=MESH)

    mine = pl.ds(pl.multiple_of(core * (rows // 2), 16), rows // 2)

    def sel_remote(hop, way):
        origin = sel_buf.at[z - way * hop, mine]
        return pltpu.make_async_remote_copy(
            origin, origin, sel_send.at[hop, (way + 1) // 2], sel_recv.at[z - way * hop],
            device_id={"occ": z + way}, device_id_type=MESH)

    def sel_pass(hop, way):
        origin = sel_buf.at[z - way * hop, mine]
        return pltpu.make_async_remote_copy(
            origin, origin, pass_send, pass_recv.at[z - way * hop],
            device_id={"pair": other}, device_id_type=MESH)

    def sel_arrival(sem, origin, half):
        block = sel_buf.at[origin, half]
        return pltpu.make_async_remote_copy(
            block, block, sel_send.at[0, 0], sem.at[origin],
            device_id={"pair": other}, device_id_type=MESH)

    def inside(place):
        return (place >= 0) & (place < n_occ)

    def rs_remote(s, t):
        return pltpu.make_async_remote_copy(
            part.at[(t, *send[s])], landed[s].at[t], rs_send.at[s], rs_recv.at[s, t],
            device_id={"pair": partner[s]}, device_id_type=MESH)

    def rs_piece(t, q):
        if pieces == 1:
            return rs_remote(0, t)
        cols = slice(q * piece, (q + 1) * piece)
        return pltpu.make_async_remote_copy(
            part.at[t, send[0][0], cols], landed[0].at[t, :, cols], rs_send.at[0], rs_recv.at[0, t],
            device_id={"pair": partner[0]}, device_id_type=MESH)

    def ag_remote(s, t):
        return pltpu.make_async_remote_copy(
            gathered.at[(t, *keep[s])], gathered.at[(t, *keep[s])], ag_send.at[s], ag_recv.at[s, t],
            device_id={"pair": partner[s]}, device_id_type=MESH)

    def ag_arrival(s, t):
        return pltpu.make_async_remote_copy(
            gathered.at[(t, *send[s])], gathered.at[(t, *send[s])], ag_send.at[s], ag_recv.at[s, t],
            device_id={"pair": partner[s]}, device_id_type=MESH)

    def twin_part(t, region):
        return pltpu.make_async_remote_copy(
            gathered.at[(t, *region)], twin.at[(t, *region)], twin_send, twin_recv.at[t],
            device_id={"pair": other}, device_id_type=MESH)

    def twin_remote(t):
        return pltpu.make_async_remote_copy(
            gathered.at[t], twin.at[t], twin_send, twin_recv.at[t],
            device_id={"pair": other}, device_id_type=MESH)

    def coef_copy(k):
        src = coef_hbm.at[:, pl.ds(pl.multiple_of(k * 128, 128), 128)]
        return pltpu.make_async_copy(src, coef_buf.at[k], coef_sem)

    virt_copy = pltpu.make_async_copy(virt_hbm, virt_buf, virt_sem)

    barrier = pltpu.get_barrier_semaphore()
    pl.semaphore_signal(barrier, inc=1, device_id={"pair": other}, device_id_type=MESH)
    for s in range(steps):
        pl.semaphore_signal(barrier, inc=1, device_id={"pair": partner[s]}, device_id_type=MESH)
    for way in (-1, 1):
        @pl.when(inside(z + way))
        def _():
            pl.semaphore_signal(barrier, inc=1, device_id={"occ": z + way}, device_id_type=MESH)

    tiles = coef_buf.shape[0]
    names = [
        pltpu.make_async_copy(screen_hbm, screen_ref, name_sem.at[0]),
        pltpu.make_async_copy(slot_hbm, slot_ref, name_sem.at[1]),
    ]
    for copy in names:
        copy.start()

    def fetch(k, _):
        coef_copy(k).start()
        return 0

    lax.fori_loop(0, tiles, fetch, 0)
    for k in range(subs):
        half_copy(k).start()

    pl.semaphore_wait(barrier, 1 + steps + inside(z - 1).astype(jnp.int32) + inside(z + 1).astype(jnp.int32))
    for k in range(subs):
        for q in range(pieces):
            half_remote(k, q).start()

    for copy in names:
        copy.wait()
    pltpu.make_async_copy(coef_buf, coef_buf, coef_sem).wait()

    per = 128 // block
    slots = 2 * depth // block
    chip = lax.div(me, 2)
    lane = lax.broadcasted_iota(jnp.int32, (rows, 128), 1)
    for pos in range(slots // per):
        tile = jnp.zeros((rows, 128), jnp.float32)
        for spot in range(per):
            name = slot_ref[chip * slots + pos * per + spot]
            keepit = screen_ref[name].astype(jnp.float32)
            at = lax.rem(name, per)
            got = coef_buf[lax.div(name, per)].astype(jnp.float32) * keepit
            for shift in range(per):
                moved = pltpu.roll(got, shift * block, 1) if shift else got
                here = (lax.rem(at + shift, per) == spot).astype(jnp.float32)
                tile = tile + jnp.where(lax.div(lane, block) == spot, moved, 0.0) * here
        sel_buf[z, :, pos * 128:(pos + 1) * 128] = tile.astype(jnp.bfloat16)

    for way in (-1, 1):
        @pl.when(inside(z + way))
        def _():
            sel_remote(0, way).start()

    def relay(hop):
        for way in (-1, 1):
            origin = z - way * hop

            @pl.when(inside(origin))
            def _():
                sel_arrival(sel_recv, origin, mine).wait_recv()

                @pl.when(inside(z + way))
                def _():
                    sel_remote(hop, way).start()

                sel_pass(hop, way).start()

    def produce(t):
        d, k = lax.div(t, subs), lax.rem(t, subs)

        origin = xor(z, d, (n_occ - 1).bit_length())

        @pl.when(t == 0)
        def _():
            for k in range(subs):
                half_copy(k).wait()

        def make(q, part_of):
            cols = slice(q * part_of, (q + 1) * part_of)
            p = jnp.dot(sel_buf[origin], half_buf[k, :, cols], preferred_element_type=jnp.float32)
            kept[t, :, cols] = p
            part[t, :, cols] = p.astype(jnp.bfloat16)

        @pl.when((d > 0) & (k == 0))
        def _():
            theirs = pl.ds(pl.multiple_of((1 - core) * (rows // 2), 16), rows // 2)
            sel_arrival(pass_recv, origin, theirs).wait_recv()

        @pl.when(t < subs + EARLY)
        def _():
            for q in range(pieces):
                if q == pieces - 1 and n_occ > 1:
                    @pl.when(t == subs - 1)
                    def _():
                        relay(1)

                @pl.when(d == 0)
                def _():
                    half_remote(k, q).wait_recv()

                make(q, piece)
                rs_piece(t, q).start()

        @pl.when(t >= subs + EARLY)
        def _():
            make(0, width)
            rs_remote(0, t).start()

    def reduce(s, t):
        rs_remote(s, t).wait_recv()
        v = kept[(t, *keep[s])] + landed[s][t].astype(jnp.float32)
        if s + 1 < steps:
            kept[(t, *keep[s])] = v
            part[(t, *keep[s])] = v.astype(jnp.bfloat16)
            rs_remote(s + 1, t).start()
        else:
            gathered[(t, *keep[s])] = v.astype(jnp.bfloat16)
            ag_remote(s, t).start()
            twin_part(t, keep[s]).start()

    def fold(t, buf, side):
        d, k = lax.div(t, subs), lax.rem(t, subs)
        cols = pl.ds(pl.multiple_of(side * half_n + k * width, 128), width)
        total[d] += lax.dot_general(
            virt_buf[:, cols], buf[t], (((1,), (1,)), ((), ())), preferred_element_type=jnp.float32)

    def gather(s, t):
        ag_arrival(s, t).wait_recv()
        if s > 0:
            ag_remote(s - 1, t).start()
        twin_part(t, send[s]).start()
        if s == 0:
            fold(t, gathered, core)

    def finish(t):
        twin_remote(t).wait_recv()
        fold(t, twin, 1 - core)
        d, k = lax.div(t, subs), lax.rem(t, subs)
        origin = xor(z, d, (n_occ - 1).bit_length())

        @pl.when(k == subs - 1)
        def _():
            if len(out_ref.shape) == 2:
                cols = pl.ds(pl.multiple_of(origin * rows, 128), rows)
                out_ref[:, cols] = total[d].astype(jnp.bfloat16)
            else:
                out_ref[origin] = total[d].astype(jnp.bfloat16)

    stages = [functools.partial(reduce, s) for s in range(steps)]
    stages += [functools.partial(gather, s) for s in reversed(range(steps))]
    stages += [finish]
    gaps = [REDUCE[min(s, 1)] for s in range(steps)]
    gaps += [GATHER[0]] + [GATHER[1]] * (steps - 1) + [FINISH]
    delay = [sum(gaps[:i + 1]) for i in range(len(gaps))]

    def body(t, _):
        @pl.when(t < chunks)
        def _():
            produce(t)

        @pl.when(t == subs)
        def _():
            virt_copy.start()
            total[...] = jnp.zeros_like(total)

        @pl.when(t == delay[-2])
        def _():
            virt_copy.wait()

        for stage, late in zip(stages, delay):
            u = t - late

            @pl.when((u >= 0) & (u < chunks))
            def _():
                stage(u)

        for hop in range(2, n_occ):
            @pl.when(t == hop * subs - 1)
            def _():
                relay(hop)
        return 0

    lax.fori_loop(0, chunks + delay[-1], body, 0)

    half_all = half_hbm.at[:, pl.ds(0, half_n)]
    pltpu.make_async_remote_copy(
        half_all, half_all, half_send, half_recv.at[0], device_id={"pair": other}, device_id_type=MESH).wait_send()
    for hop in range(n_occ):
        for way in (-1, 1):
            @pl.when(inside(z - way * hop) & inside(z + way))
            def _():
                sel_remote(hop, way).wait_send()

    passed = sel_buf.at[pl.ds(0, n_occ - 1), mine]
    pltpu.make_async_remote_copy(
        passed, passed, pass_send, pass_recv.at[0], device_id={"pair": other}, device_id_type=MESH).wait_send()
    for s in range(steps):
        for sem in (rs_send, ag_send):
            pltpu.make_async_remote_copy(
                landed[s], landed[s], sem.at[s], rs_recv.at[s, 0],
                device_id={"pair": partner[s]}, device_id_type=MESH).wait_send()
    pltpu.make_async_remote_copy(
        gathered, twin, twin_send, twin_recv.at[0], device_id={"pair": other}, device_id_type=MESH).wait_send()


def shards(n_pair, n_occ, half_ints, pair_coef, mo_virtual, screen, slot_block):
    rows = pair_coef.shape[0]
    basis = half_ints.shape[2]
    depth = half_ints.shape[1]
    half_ints = half_ints.reshape(depth, basis)
    block = pair_coef.shape[1] // screen.shape[0]
    width = min(WIDTH, basis // 2)
    subs = basis // 2 // width
    chunks = subs * n_occ
    virt = mo_virtual.shape[0]
    steps = n_pair.bit_length() - 2
    tiles = pair_coef.shape[1] // 128
    wide = rows % 128 == 0
    landed = []
    r, c = rows, width
    for _ in range(steps):
        r, c = (r // 2, c) if r >= 32 else (r, c // 2)
        landed.append(pltpu.VMEM((chunks, r, c), jnp.bfloat16))
    dma = pltpu.SemaphoreType.DMA
    out = pl.pallas_call(
        functools.partial(kernel, n_pair, n_occ, block),
        out_shape=pltpu.VMEM(
            (virt, n_occ * rows) if wide else (n_occ, virt, rows), jnp.bfloat16),
        in_specs=[pl.BlockSpec(memory_space=pltpu.HBM)] * 5,
        out_specs=pl.BlockSpec(memory_space=pltpu.VMEM),
        scratch_shapes=[
            pltpu.VMEM((tiles, rows, 128), jnp.bfloat16),
            pltpu.VMEM((subs, 2 * depth, width), jnp.bfloat16),
            pltpu.VMEM((n_occ, rows, 2 * depth), jnp.bfloat16),
            pltpu.VMEM((virt, basis), jnp.bfloat16),
            pltpu.VMEM((chunks, rows, width), jnp.bfloat16),
            pltpu.VMEM((chunks, rows, width), jnp.float32),
            pltpu.VMEM((chunks, rows, width), jnp.bfloat16),
            pltpu.VMEM((chunks, rows, width), jnp.bfloat16),
            pltpu.VMEM((n_occ, virt, rows), jnp.float32),
            pltpu.SMEM(screen.shape, jnp.int32),
            pltpu.SMEM(slot_block.shape, jnp.int32),
            *landed,
            dma((2,)), dma, dma, dma, dma((subs * (width // PIECE if rows >= 32 and width % PIECE == 0 else 1),)),
            dma((n_occ, 2)), dma((n_occ,)), dma, dma((n_occ,)), dma,
            dma((steps,)), dma((steps, chunks)), dma((steps,)), dma((steps, chunks)),
            dma, dma((chunks,)),
        ],
        compiler_params=pltpu.CompilerParams(
            collective_id=0, has_side_effects=True, vmem_limit_bytes=VMEM),
    )(half_ints, pair_coef, mo_virtual, screen, slot_block)
    if not wide:
        out = jnp.transpose(out, (1, 0, 2))
    return out.reshape(virt, 1, n_occ * rows)


def solution(mesh):
    placed = (P("occ", "pair", None), P("occ", None), P("pair", None), P(), P())
    return jax.shard_map(
        functools.partial(shards, mesh.shape["pair"], mesh.shape["occ"]),
        mesh=mesh, in_specs=placed, out_specs=P("pair", "occ", None), check_vma=False,
    )
```

```python
import functools

import jax
import jax.numpy as jnp
from jax import lax
from jax.experimental import pallas as pl
from jax.experimental.pallas import tpu as pltpu
from jax.sharding import PartitionSpec as P

MESH = pl.DeviceIdType.MESH
WIDTH = 1024
PIECE = 256
VMEM = 56 * 2**20
REDUCE = 2, 3
GATHER = 3, 3
FINISH = 1


def flip(index, stride):
    return index + stride * (1 - 2 * (lax.rem(lax.div(index, stride), 2)))


def flip_by(index, mask):
    for bit in range(mask.bit_length()):
        if (mask >> bit) & 1:
            index = flip(index, 1 << bit)
    return index


def xor(a, b, bits):
    total = 0
    for bit in range(bits):
        total = total + lax.rem(lax.div(a, 1 << bit) + lax.div(b, 1 << bit), 2) * (1 << bit)
    return total


def kernel(
    n_pair, n_occ, block,
    half_hbm, coef_hbm, virt_hbm, screen_hbm, slot_hbm,
    out_ref,
    coef_buf, half_buf, sel_buf, virt_buf, part, kept, gathered, twin, total,
    screen_ref, slot_ref, *rest,
):
    steps = n_pair.bit_length() - 2
    landed, sems = rest[:steps], rest[steps:]
    (name_sem, coef_sem, half_local, half_send, half_recv, sel_send, sel_recv, pass_send, pass_recv,
     virt_sem, rs_send, rs_recv, ag_send, ag_recv, twin_send, twin_recv) = sems
    me = lax.axis_index("pair")
    z = lax.axis_index("occ")
    core = lax.rem(me, 2)
    other = flip(me, 1)
    subs, _, width = half_buf.shape
    chunks, rows, _ = part.shape
    depth = half_hbm.shape[0]
    half_n = subs * width

    up = [2 << s for s in range(steps)]
    down = up[steps // 2:] + up[:steps // 2]
    stride = [a + core * (b - a) for a, b in zip(up, down)]
    partner = [flip(me, s) for s in stride]
    keep, send = [], []
    r0, c0, r, c = 0, 0, rows, width
    for s in range(steps):
        bit = lax.rem(lax.div(me, stride[s]), 2)
        if r >= 32:
            r = r // 2
            kr, kc, sr, sc = r0 + bit * r, c0, r0 + (1 - bit) * r, c0
        else:
            c = c // 2
            kr, kc, sr, sc = r0, c0 + bit * c, r0, c0 + (1 - bit) * c
        region = lambda a, b, r=r, c=c: (
            pl.ds(a if isinstance(a, int) else pl.multiple_of(a, 16), r),
            pl.ds(b if isinstance(b, int) else pl.multiple_of(b, 128), c),
        )
        keep.append(region(kr, kc))
        send.append(region(sr, sc))
        r0, c0 = kr, kc

    def half_copy(k):
        own = half_hbm.at[:, pl.ds(pl.multiple_of(core * half_n + k * width, 128), width)]
        dst = half_buf.at[k, pl.ds(pl.multiple_of(core * depth, 16), depth), :]
        return pltpu.make_async_copy(own, dst, half_local)

    pieces = half_recv.shape[0] // subs
    piece = width // pieces

    def half_remote(k, q):
        src = half_hbm.at[:, pl.ds(pl.multiple_of((1 - core) * half_n + k * width + q * piece, 128), piece)]
        dst = half_buf.at[k, pl.ds(pl.multiple_of(core * depth, 16), depth), q * piece:(q + 1) * piece]
        return pltpu.make_async_remote_copy(
            src, dst, half_send, half_recv.at[k * pieces + q], device_id={"pair": other}, device_id_type=MESH)

    mine = pl.ds(pl.multiple_of(core * (rows // 2), 16), rows // 2)

    def sel_remote(hop, way):
        origin = sel_buf.at[z - way * hop, mine]
        return pltpu.make_async_remote_copy(
            origin, origin, sel_send.at[hop, (way + 1) // 2], sel_recv.at[z - way * hop],
            device_id={"occ": z + way}, device_id_type=MESH)

    def sel_pass(hop, way):
        origin = sel_buf.at[z - way * hop, mine]
        return pltpu.make_async_remote_copy(
            origin, origin, pass_send, pass_recv.at[z - way * hop],
            device_id={"pair": other}, device_id_type=MESH)

    def sel_arrival(sem, origin, half):
        block = sel_buf.at[origin, half]
        return pltpu.make_async_remote_copy(
            block, block, sel_send.at[0, 0], sem.at[origin],
            device_id={"pair": other}, device_id_type=MESH)

    def inside(place):
        return (place >= 0) & (place < n_occ)

    def rs_remote(s, t):
        return pltpu.make_async_remote_copy(
            part.at[(t, *send[s])], landed[s].at[t], rs_send.at[s], rs_recv.at[s, t],
            device_id={"pair": partner[s]}, device_id_type=MESH)

    def rs_piece(t, q):
        if pieces == 1:
            return rs_remote(0, t)
        cols = slice(q * piece, (q + 1) * piece)
        return pltpu.make_async_remote_copy(
            part.at[t, send[0][0], cols], landed[0].at[t, :, cols], rs_send.at[0], rs_recv.at[0, t],
            device_id={"pair": partner[0]}, device_id_type=MESH)

    def ag_remote(s, t):
        return pltpu.make_async_remote_copy(
            gathered.at[(t, *keep[s])], gathered.at[(t, *keep[s])], ag_send.at[s], ag_recv.at[s, t],
            device_id={"pair": partner[s]}, device_id_type=MESH)

    def ag_arrival(s, t):
        return pltpu.make_async_remote_copy(
            gathered.at[(t, *send[s])], gathered.at[(t, *send[s])], ag_send.at[s], ag_recv.at[s, t],
            device_id={"pair": partner[s]}, device_id_type=MESH)

    def twin_part(t, region):
        return pltpu.make_async_remote_copy(
            gathered.at[(t, *region)], twin.at[(t, *region)], twin_send, twin_recv.at[t],
            device_id={"pair": other}, device_id_type=MESH)

    def twin_remote(t):
        return pltpu.make_async_remote_copy(
            gathered.at[t], twin.at[t], twin_send, twin_recv.at[t],
            device_id={"pair": other}, device_id_type=MESH)

    def coef_copy(k):
        src = coef_hbm.at[:, pl.ds(pl.multiple_of(k * 128, 128), 128)]
        return pltpu.make_async_copy(src, coef_buf.at[k], coef_sem)

    virt_copy = pltpu.make_async_copy(virt_hbm, virt_buf, virt_sem)

    barrier = pltpu.get_barrier_semaphore()
    pl.semaphore_signal(barrier, inc=1, device_id={"pair": other}, device_id_type=MESH)
    for s in range(steps):
        pl.semaphore_signal(barrier, inc=1, device_id={"pair": partner[s]}, device_id_type=MESH)
    for way in (-1, 1):
        @pl.when(inside(z + way))
        def _():
            pl.semaphore_signal(barrier, inc=1, device_id={"occ": z + way}, device_id_type=MESH)

    tiles = coef_buf.shape[0]
    names = [
        pltpu.make_async_copy(screen_hbm, screen_ref, name_sem.at[0]),
        pltpu.make_async_copy(slot_hbm, slot_ref, name_sem.at[1]),
    ]
    for copy in names:
        copy.start()

    def fetch(k, _):
        coef_copy(k).start()
        return 0

    lax.fori_loop(0, tiles, fetch, 0)
    for k in range(subs):
        half_copy(k).start()

    pl.semaphore_wait(barrier, 1 + steps + inside(z - 1).astype(jnp.int32) + inside(z + 1).astype(jnp.int32))
    for k in range(subs):
        for q in range(pieces):
            half_remote(k, q).start()

    for copy in names:
        copy.wait()
    pltpu.make_async_copy(coef_buf, coef_buf, coef_sem).wait()

    per = 128 // block
    slots = 2 * depth // block
    chip = lax.div(me, 2)
    lane = lax.broadcasted_iota(jnp.int32, (rows, 128), 1)
    for pos in range(slots // per):
        tile = jnp.zeros((rows, 128), jnp.float32)
        for spot in range(per):
            name = slot_ref[chip * slots + pos * per + spot]
            keepit = screen_ref[name].astype(jnp.float32)
            at = lax.rem(name, per)
            got = coef_buf[lax.div(name, per)].astype(jnp.float32) * keepit
            for shift in range(per):
                moved = pltpu.roll(got, shift * block, 1) if shift else got
                here = (lax.rem(at + shift, per) == spot).astype(jnp.float32)
                tile = tile + jnp.where(lax.div(lane, block) == spot, moved, 0.0) * here
        sel_buf[z, :, pos * 128:(pos + 1) * 128] = tile.astype(jnp.bfloat16)

    for way in (-1, 1):
        @pl.when(inside(z + way))
        def _():
            sel_remote(0, way).start()

    def relay(hop):
        for way in (-1, 1):
            origin = z - way * hop

            @pl.when(inside(origin))
            def _():
                sel_arrival(sel_recv, origin, mine).wait_recv()

                @pl.when(inside(z + way))
                def _():
                    sel_remote(hop, way).start()

                sel_pass(hop, way).start()

    def produce(t):
        d, k = lax.div(t, subs), lax.rem(t, subs)

        origin = xor(z, d, (n_occ - 1).bit_length())

        @pl.when(t == 0)
        def _():
            for k in range(subs):
                half_copy(k).wait()

        def make(q, part_of):
            cols = slice(q * part_of, (q + 1) * part_of)
            p = jnp.dot(sel_buf[origin], half_buf[k, :, cols], preferred_element_type=jnp.float32)
            kept[t, :, cols] = p
            part[t, :, cols] = p.astype(jnp.bfloat16)

        @pl.when((d > 0) & (k == 0))
        def _():
            theirs = pl.ds(pl.multiple_of((1 - core) * (rows // 2), 16), rows // 2)
            sel_arrival(pass_recv, origin, theirs).wait_recv()

        for q in range(pieces):
            if q == pieces - 1 and n_occ > 1:
                @pl.when(t == subs - 1)
                def _():
                    relay(1)

            @pl.when(d == 0)
            def _():
                half_remote(k, q).wait_recv()

            make(q, piece)
            rs_piece(t, q).start()

    def reduce(s, t):
        rs_remote(s, t).wait_recv()
        v = kept[(t, *keep[s])] + landed[s][t].astype(jnp.float32)
        if s + 1 < steps:
            kept[(t, *keep[s])] = v
            part[(t, *keep[s])] = v.astype(jnp.bfloat16)
            rs_remote(s + 1, t).start()
        else:
            gathered[(t, *keep[s])] = v.astype(jnp.bfloat16)
            ag_remote(s, t).start()
            twin_part(t, keep[s]).start()

    def fold(t, buf, side):
        d, k = lax.div(t, subs), lax.rem(t, subs)
        cols = pl.ds(pl.multiple_of(side * half_n + k * width, 128), width)
        total[d] += lax.dot_general(
            virt_buf[:, cols], buf[t], (((1,), (1,)), ((), ())), preferred_element_type=jnp.float32)

    def gather(s, t):
        ag_arrival(s, t).wait_recv()
        if s > 0:
            ag_remote(s - 1, t).start()
        twin_part(t, send[s]).start()
        if s == 0:
            fold(t, gathered, core)

    def finish(t):
        twin_remote(t).wait_recv()
        fold(t, twin, 1 - core)
        d, k = lax.div(t, subs), lax.rem(t, subs)
        origin = xor(z, d, (n_occ - 1).bit_length())

        @pl.when(k == subs - 1)
        def _():
            if len(out_ref.shape) == 2:
                cols = pl.ds(pl.multiple_of(origin * rows, 128), rows)
                out_ref[:, cols] = total[d].astype(jnp.bfloat16)
            else:
                out_ref[origin] = total[d].astype(jnp.bfloat16)

    stages = [functools.partial(reduce, s) for s in range(steps)]
    stages += [functools.partial(gather, s) for s in reversed(range(steps))]
    stages += [finish]
    gaps = [REDUCE[min(s, 1)] for s in range(steps)]
    gaps += [GATHER[0]] + [GATHER[1]] * (steps - 1) + [FINISH]
    delay = [sum(gaps[:i + 1]) for i in range(len(gaps))]

    def body(t, _):
        @pl.when(t < chunks)
        def _():
            produce(t)

        @pl.when(t == subs)
        def _():
            virt_copy.start()
            total[...] = jnp.zeros_like(total)

        @pl.when(t == delay[-2])
        def _():
            virt_copy.wait()

        for stage, late in zip(stages, delay):
            u = t - late

            @pl.when((u >= 0) & (u < chunks))
            def _():
                stage(u)

        for hop in range(2, n_occ):
            @pl.when(t == hop * subs - 1)
            def _():
                relay(hop)
        return 0

    lax.fori_loop(0, chunks + delay[-1], body, 0)

    half_all = half_hbm.at[:, pl.ds(0, half_n)]
    pltpu.make_async_remote_copy(
        half_all, half_all, half_send, half_recv.at[0], device_id={"pair": other}, device_id_type=MESH).wait_send()
    for hop in range(n_occ):
        for way in (-1, 1):
            @pl.when(inside(z - way * hop) & inside(z + way))
            def _():
                sel_remote(hop, way).wait_send()

    passed = sel_buf.at[pl.ds(0, n_occ - 1), mine]
    pltpu.make_async_remote_copy(
        passed, passed, pass_send, pass_recv.at[0], device_id={"pair": other}, device_id_type=MESH).wait_send()
    for s in range(steps):
        for sem in (rs_send, ag_send):
            pltpu.make_async_remote_copy(
                landed[s], landed[s], sem.at[s], rs_recv.at[s, 0],
                device_id={"pair": partner[s]}, device_id_type=MESH).wait_send()
    pltpu.make_async_remote_copy(
        gathered, twin, twin_send, twin_recv.at[0], device_id={"pair": other}, device_id_type=MESH).wait_send()


def shards(n_pair, n_occ, half_ints, pair_coef, mo_virtual, screen, slot_block):
    rows = pair_coef.shape[0]
    basis = half_ints.shape[2]
    depth = half_ints.shape[1]
    half_ints = half_ints.reshape(depth, basis)
    block = pair_coef.shape[1] // screen.shape[0]
    width = min(WIDTH, basis // 2)
    subs = basis // 2 // width
    chunks = subs * n_occ
    virt = mo_virtual.shape[0]
    steps = n_pair.bit_length() - 2
    tiles = pair_coef.shape[1] // 128
    wide = rows % 128 == 0
    landed = []
    r, c = rows, width
    for _ in range(steps):
        r, c = (r // 2, c) if r >= 32 else (r, c // 2)
        landed.append(pltpu.VMEM((chunks, r, c), jnp.bfloat16))
    dma = pltpu.SemaphoreType.DMA
    out = pl.pallas_call(
        functools.partial(kernel, n_pair, n_occ, block),
        out_shape=pltpu.VMEM(
            (virt, n_occ * rows) if wide else (n_occ, virt, rows), jnp.bfloat16),
        in_specs=[pl.BlockSpec(memory_space=pltpu.HBM)] * 5,
        out_specs=pl.BlockSpec(memory_space=pltpu.VMEM),
        scratch_shapes=[
            pltpu.VMEM((tiles, rows, 128), jnp.bfloat16),
            pltpu.VMEM((subs, 2 * depth, width), jnp.bfloat16),
            pltpu.VMEM((n_occ, rows, 2 * depth), jnp.bfloat16),
            pltpu.VMEM((virt, basis), jnp.bfloat16),
            pltpu.VMEM((chunks, rows, width), jnp.bfloat16),
            pltpu.VMEM((chunks, rows, width), jnp.float32),
            pltpu.VMEM((chunks, rows, width), jnp.bfloat16),
            pltpu.VMEM((chunks, rows, width), jnp.bfloat16),
            pltpu.VMEM((n_occ, virt, rows), jnp.float32),
            pltpu.SMEM(screen.shape, jnp.int32),
            pltpu.SMEM(slot_block.shape, jnp.int32),
            *landed,
            dma((2,)), dma, dma, dma, dma((subs * (width // PIECE if rows >= 32 and width % PIECE == 0 else 1),)),
            dma((n_occ, 2)), dma((n_occ,)), dma, dma((n_occ,)), dma,
            dma((steps,)), dma((steps, chunks)), dma((steps,)), dma((steps, chunks)),
            dma, dma((chunks,)),
        ],
        compiler_params=pltpu.CompilerParams(
            collective_id=0, has_side_effects=True, vmem_limit_bytes=VMEM),
    )(half_ints, pair_coef, mo_virtual, screen, slot_block)
    if not wide:
        out = jnp.transpose(out, (1, 0, 2))
    return out.reshape(virt, 1, n_occ * rows)


def solution(mesh):
    placed = (P("occ", "pair", None), P("occ", None), P("pair", None), P(), P())
    return jax.shard_map(
        functools.partial(shards, mesh.shape["pair"], mesh.shape["occ"]),
        mesh=mesh, in_specs=placed, out_specs=P("pair", "occ", None), check_vma=False,
    )
```

```python
import functools

import jax
import jax.numpy as jnp
from jax import lax
from jax.experimental import pallas as pl
from jax.experimental.pallas import tpu as pltpu
from jax.sharding import PartitionSpec as P

MESH = pl.DeviceIdType.MESH
WIDTH = 1024
PIECE = 256
EARLY = 1
VMEM = 56 * 2**20
REDUCE = 2, 3
GATHER = 3, 3
FINISH = 1


def flip(index, stride):
    return index + stride * (1 - 2 * (lax.rem(lax.div(index, stride), 2)))


def flip_by(index, mask):
    for bit in range(mask.bit_length()):
        if (mask >> bit) & 1:
            index = flip(index, 1 << bit)
    return index


def xor(a, b, bits):
    total = 0
    for bit in range(bits):
        total = total + lax.rem(lax.div(a, 1 << bit) + lax.div(b, 1 << bit), 2) * (1 << bit)
    return total


def kernel(
    n_pair, n_occ, block,
    half_hbm, coef_hbm, virt_hbm, screen_hbm, slot_hbm,
    out_ref,
    coef_buf, half_buf, sel_buf, virt_buf, part, kept, gathered, twin, total,
    screen_ref, slot_ref, *rest,
):
    steps = n_pair.bit_length() - 2
    landed, sems = rest[:steps], rest[steps:]
    (name_sem, coef_sem, half_local, half_send, half_recv, sel_send, sel_recv, pass_send, pass_recv,
     virt_sem, rs_send, rs_recv, ag_send, ag_recv, twin_send, twin_recv) = sems
    me = lax.axis_index("pair")
    z = lax.axis_index("occ")
    core = lax.rem(me, 2)
    other = flip(me, 1)
    subs, _, width = half_buf.shape
    chunks, rows, _ = part.shape
    depth = half_hbm.shape[0]
    half_n = subs * width
    ring = rs_recv.shape[1]

    up = [2 << s for s in range(steps)]
    down = up[steps // 2:] + up[:steps // 2]
    stride = [a + core * (b - a) for a, b in zip(up, down)]
    partner = [flip(me, s) for s in stride]
    keep, send = [], []
    r0, c0, r, c = 0, 0, rows, width
    for s in range(steps):
        bit = lax.rem(lax.div(me, stride[s]), 2)
        if r >= 32:
            r = r // 2
            kr, kc, sr, sc = r0 + bit * r, c0, r0 + (1 - bit) * r, c0
        else:
            c = c // 2
            kr, kc, sr, sc = r0, c0 + bit * c, r0, c0 + (1 - bit) * c
        region = lambda a, b, r=r, c=c: (
            pl.ds(a if isinstance(a, int) else pl.multiple_of(a, 16), r),
            pl.ds(b if isinstance(b, int) else pl.multiple_of(b, 128), c),
        )
        keep.append(region(kr, kc))
        send.append(region(sr, sc))
        r0, c0 = kr, kc

    def half_copy(k):
        own = half_hbm.at[:, pl.ds(pl.multiple_of(core * half_n + k * width, 128), width)]
        dst = half_buf.at[k, pl.ds(pl.multiple_of(core * depth, 16), depth), :]
        return pltpu.make_async_copy(own, dst, half_local)

    pieces = half_recv.shape[0] // subs
    piece = width // pieces

    def half_remote(k, q):
        src = half_hbm.at[:, pl.ds(pl.multiple_of((1 - core) * half_n + k * width + q * piece, 128), piece)]
        dst = half_buf.at[k, pl.ds(pl.multiple_of(core * depth, 16), depth), q * piece:(q + 1) * piece]
        return pltpu.make_async_remote_copy(
            src, dst, half_send, half_recv.at[k * pieces + q], device_id={"pair": other}, device_id_type=MESH)

    mine = pl.ds(pl.multiple_of(core * (rows // 2), 16), rows // 2)

    def sel_remote(hop, way):
        origin = sel_buf.at[z - way * hop, mine]
        return pltpu.make_async_remote_copy(
            origin, origin, sel_send.at[hop, (way + 1) // 2], sel_recv.at[z - way * hop],
            device_id={"occ": z + way}, device_id_type=MESH)

    def sel_pass(hop, way):
        origin = sel_buf.at[z - way * hop, mine]
        return pltpu.make_async_remote_copy(
            origin, origin, pass_send, pass_recv.at[z - way * hop],
            device_id={"pair": other}, device_id_type=MESH)

    def sel_arrival(sem, origin, half):
        block = sel_buf.at[origin, half]
        return pltpu.make_async_remote_copy(
            block, block, sel_send.at[0, 0], sem.at[origin],
            device_id={"pair": other}, device_id_type=MESH)

    def inside(place):
        return (place >= 0) & (place < n_occ)

    def rs_remote(s, t):
        return pltpu.make_async_remote_copy(
            part.at[(t, *send[s])], landed[s].at[t], rs_send.at[s], rs_recv.at[s, lax.rem(t, ring)],
            device_id={"pair": partner[s]}, device_id_type=MESH)

    def rs_piece(t, q):
        if pieces == 1:
            return rs_remote(0, t)
        cols = slice(q * piece, (q + 1) * piece)
        return pltpu.make_async_remote_copy(
            part.at[t, send[0][0], cols], landed[0].at[t, :, cols], rs_send.at[0], rs_recv.at[0, lax.rem(t, ring)],
            device_id={"pair": partner[0]}, device_id_type=MESH)

    def ag_remote(s, t):
        return pltpu.make_async_remote_copy(
            gathered.at[(t, *keep[s])], gathered.at[(t, *keep[s])], ag_send.at[s], ag_recv.at[s, lax.rem(t, ring)],
            device_id={"pair": partner[s]}, device_id_type=MESH)

    def ag_arrival(s, t):
        return pltpu.make_async_remote_copy(
            gathered.at[(t, *send[s])], gathered.at[(t, *send[s])], ag_send.at[s], ag_recv.at[s, lax.rem(t, ring)],
            device_id={"pair": partner[s]}, device_id_type=MESH)

    def twin_part(t, region):
        return pltpu.make_async_remote_copy(
            gathered.at[(t, *region)], twin.at[(t, *region)], twin_send, twin_recv.at[t],
            device_id={"pair": other}, device_id_type=MESH)

    def twin_remote(t):
        return pltpu.make_async_remote_copy(
            gathered.at[t], twin.at[t], twin_send, twin_recv.at[t],
            device_id={"pair": other}, device_id_type=MESH)

    def coef_copy(k):
        src = coef_hbm.at[:, pl.ds(pl.multiple_of(k * 128, 128), 128)]
        return pltpu.make_async_copy(src, coef_buf.at[k], coef_sem)

    virt_copy = pltpu.make_async_copy(virt_hbm, virt_buf, virt_sem)

    barrier = pltpu.get_barrier_semaphore()
    pl.semaphore_signal(barrier, inc=1, device_id={"pair": other}, device_id_type=MESH)
    for s in range(steps):
        pl.semaphore_signal(barrier, inc=1, device_id={"pair": partner[s]}, device_id_type=MESH)
    for way in (-1, 1):
        @pl.when(inside(z + way))
        def _():
            pl.semaphore_signal(barrier, inc=1, device_id={"occ": z + way}, device_id_type=MESH)

    tiles = coef_buf.shape[0]
    names = [
        pltpu.make_async_copy(screen_hbm, screen_ref, name_sem.at[0]),
        pltpu.make_async_copy(slot_hbm, slot_ref, name_sem.at[1]),
    ]
    for copy in names:
        copy.start()

    def fetch(k, _):
        coef_copy(k).start()
        return 0

    lax.fori_loop(0, tiles, fetch, 0)
    for k in range(subs):
        half_copy(k).start()

    pl.semaphore_wait(barrier, 1 + steps + inside(z - 1).astype(jnp.int32) + inside(z + 1).astype(jnp.int32))
    for k in range(subs):
        for q in range(pieces):
            half_remote(k, q).start()

    for copy in names:
        copy.wait()
    pltpu.make_async_copy(coef_buf, coef_buf, coef_sem).wait()

    per = 128 // block
    slots = 2 * depth // block
    chip = lax.div(me, 2)
    lane = lax.broadcasted_iota(jnp.int32, (rows, 128), 1)
    for pos in range(slots // per):
        tile = jnp.zeros((rows, 128), jnp.float32)
        for spot in range(per):
            name = slot_ref[chip * slots + pos * per + spot]
            keepit = screen_ref[name].astype(jnp.float32)
            at = lax.rem(name, per)
            got = coef_buf[lax.div(name, per)].astype(jnp.float32) * keepit
            for shift in range(per):
                moved = pltpu.roll(got, shift * block, 1) if shift else got
                here = (lax.rem(at + shift, per) == spot).astype(jnp.float32)
                tile = tile + jnp.where(lax.div(lane, block) == spot, moved, 0.0) * here
        sel_buf[z, :, pos * 128:(pos + 1) * 128] = tile.astype(jnp.bfloat16)

    for way in (-1, 1):
        @pl.when(inside(z + way))
        def _():
            sel_remote(0, way).start()

    def relay(hop):
        for way in (-1, 1):
            origin = z - way * hop

            @pl.when(inside(origin))
            def _():
                sel_arrival(sel_recv, origin, mine).wait_recv()

                @pl.when(inside(z + way))
                def _():
                    sel_remote(hop, way).start()

                sel_pass(hop, way).start()

    def produce(t):
        d, k = lax.div(t, subs), lax.rem(t, subs)

        origin = xor(z, d, (n_occ - 1).bit_length())

        @pl.when(t == 0)
        def _():
            for k in range(subs):
                half_copy(k).wait()

        def make(q, part_of):
            cols = slice(q * part_of, (q + 1) * part_of)
            p = jnp.dot(sel_buf[origin], half_buf[k, :, cols], preferred_element_type=jnp.float32)
            kept[t, :, cols] = p
            part[t, :, cols] = p.astype(jnp.bfloat16)

        @pl.when((d > 0) & (k == 0))
        def _():
            theirs = pl.ds(pl.multiple_of((1 - core) * (rows // 2), 16), rows // 2)
            sel_arrival(pass_recv, origin, theirs).wait_recv()

        @pl.when(t < subs + EARLY)
        def _():
            for q in range(pieces):
                if q == pieces - 1 and n_occ > 1:
                    @pl.when(t == subs - 1)
                    def _():
                        relay(1)

                @pl.when(d == 0)
                def _():
                    half_remote(k, q).wait_recv()

                make(q, piece)
                rs_piece(t, q).start()

        @pl.when(t >= subs + EARLY)
        def _():
            make(0, width)
            rs_remote(0, t).start()

    def reduce(s, t):
        rs_remote(s, t).wait_recv()
        v = kept[(t, *keep[s])] + landed[s][t].astype(jnp.float32)
        if s + 1 < steps:
            kept[(t, *keep[s])] = v
            part[(t, *keep[s])] = v.astype(jnp.bfloat16)
            rs_remote(s + 1, t).start()
        else:
            gathered[(t, *keep[s])] = v.astype(jnp.bfloat16)
            ag_remote(s, t).start()
            twin_part(t, keep[s]).start()

    def fold(t, buf, side):
        d, k = lax.div(t, subs), lax.rem(t, subs)
        cols = pl.ds(pl.multiple_of(side * half_n + k * width, 128), width)
        total[d] += lax.dot_general(
            virt_buf[:, cols], buf[t], (((1,), (1,)), ((), ())), preferred_element_type=jnp.float32)

    def gather(s, t):
        ag_arrival(s, t).wait_recv()
        if s > 0:
            ag_remote(s - 1, t).start()
        twin_part(t, send[s]).start()
        if s == 0:
            fold(t, gathered, core)

    def finish(t):
        twin_remote(t).wait_recv()
        fold(t, twin, 1 - core)
        d, k = lax.div(t, subs), lax.rem(t, subs)
        origin = xor(z, d, (n_occ - 1).bit_length())

        @pl.when(k == subs - 1)
        def _():
            if len(out_ref.shape) == 2:
                cols = pl.ds(pl.multiple_of(origin * rows, 128), rows)
                out_ref[:, cols] = total[d].astype(jnp.bfloat16)
            else:
                out_ref[origin] = total[d].astype(jnp.bfloat16)

    stages = [functools.partial(reduce, s) for s in range(steps)]
    stages += [functools.partial(gather, s) for s in reversed(range(steps))]
    stages += [finish]
    gaps = [REDUCE[min(s, 1)] for s in range(steps)]
    gaps += [GATHER[0]] + [GATHER[1]] * (steps - 1) + [FINISH]
    delay = [sum(gaps[:i + 1]) for i in range(len(gaps))]

    def body(t, _):
        @pl.when(t < chunks)
        def _():
            produce(t)

        @pl.when(t == subs)
        def _():
            virt_copy.start()
            total[...] = jnp.zeros_like(total)

        @pl.when(t == delay[-2])
        def _():
            virt_copy.wait()

        for stage, late in zip(stages, delay):
            u = t - late

            @pl.when((u >= 0) & (u < chunks))
            def _():
                stage(u)

        for hop in range(2, n_occ):
            @pl.when(t == hop * subs - 1)
            def _():
                relay(hop)
        return 0

    lax.fori_loop(0, chunks + delay[-1], body, 0)

    half_all = half_hbm.at[:, pl.ds(0, half_n)]
    pltpu.make_async_remote_copy(
        half_all, half_all, half_send, half_recv.at[0], device_id={"pair": other}, device_id_type=MESH).wait_send()
    for hop in range(n_occ):
        for way in (-1, 1):
            @pl.when(inside(z - way * hop) & inside(z + way))
            def _():
                sel_remote(hop, way).wait_send()

    passed = sel_buf.at[pl.ds(0, n_occ - 1), mine]
    pltpu.make_async_remote_copy(
        passed, passed, pass_send, pass_recv.at[0], device_id={"pair": other}, device_id_type=MESH).wait_send()
    for s in range(steps):
        for sem in (rs_send, ag_send):
            pltpu.make_async_remote_copy(
                landed[s], landed[s], sem.at[s], rs_recv.at[s, 0],
                device_id={"pair": partner[s]}, device_id_type=MESH).wait_send()
    pltpu.make_async_remote_copy(
        gathered, twin, twin_send, twin_recv.at[0], device_id={"pair": other}, device_id_type=MESH).wait_send()


def shards(n_pair, n_occ, half_ints, pair_coef, mo_virtual, screen, slot_block):
    rows = pair_coef.shape[0]
    basis = half_ints.shape[2]
    depth = half_ints.shape[1]
    half_ints = half_ints.reshape(depth, basis)
    block = pair_coef.shape[1] // screen.shape[0]
    width = min(WIDTH, basis // 2)
    subs = basis // 2 // width
    chunks = subs * n_occ
    virt = mo_virtual.shape[0]
    steps = n_pair.bit_length() - 2
    tiles = pair_coef.shape[1] // 128
    wide = rows % 128 == 0
    ring = min(chunks, 2 * (max(*REDUCE, *GATHER) + 1))
    landed = []
    r, c = rows, width
    for _ in range(steps):
        r, c = (r // 2, c) if r >= 32 else (r, c // 2)
        landed.append(pltpu.VMEM((chunks, r, c), jnp.bfloat16))
    dma = pltpu.SemaphoreType.DMA
    out = pl.pallas_call(
        functools.partial(kernel, n_pair, n_occ, block),
        out_shape=pltpu.VMEM(
            (virt, n_occ * rows) if wide else (n_occ, virt, rows), jnp.bfloat16),
        in_specs=[pl.BlockSpec(memory_space=pltpu.HBM)] * 5,
        out_specs=pl.BlockSpec(memory_space=pltpu.VMEM),
        scratch_shapes=[
            pltpu.VMEM((tiles, rows, 128), jnp.bfloat16),
            pltpu.VMEM((subs, 2 * depth, width), jnp.bfloat16),
            pltpu.VMEM((n_occ, rows, 2 * depth), jnp.bfloat16),
            pltpu.VMEM((virt, basis), jnp.bfloat16),
            pltpu.VMEM((chunks, rows, width), jnp.bfloat16),
            pltpu.VMEM((chunks, rows, width), jnp.float32),
            pltpu.VMEM((chunks, rows, width), jnp.bfloat16),
            pltpu.VMEM((chunks, rows, width), jnp.bfloat16),
            pltpu.VMEM((n_occ, virt, rows), jnp.float32),
            pltpu.SMEM(screen.shape, jnp.int32),
            pltpu.SMEM(slot_block.shape, jnp.int32),
            *landed,
            dma((2,)), dma, dma, dma, dma((subs * (width // PIECE if rows >= 32 and width % PIECE == 0 else 1),)),
            dma((n_occ, 2)), dma((n_occ,)), dma, dma((n_occ,)), dma,
            dma((steps,)), dma((steps, ring)), dma((steps,)), dma((steps, ring)),
            dma, dma((chunks,)),
        ],
        compiler_params=pltpu.CompilerParams(
            collective_id=0, has_side_effects=True, vmem_limit_bytes=VMEM),
    )(half_ints, pair_coef, mo_virtual, screen, slot_block)
    if not wide:
        out = jnp.transpose(out, (1, 0, 2))
    return out.reshape(virt, 1, n_occ * rows)


def solution(mesh):
    placed = (P("occ", "pair", None), P("occ", None), P("pair", None), P(), P())
    return jax.shard_map(
        functools.partial(shards, mesh.shape["pair"], mesh.shape["occ"]),
        mesh=mesh, in_specs=placed, out_specs=P("pair", "occ", None), check_vma=False,
    )
```
